32 devices in a mesh: wide: 8 (over z, x), narrow: 4 (over y, core).
Axes of the slice: x: 2, y: 2, z: 4, core: 2. Of those that a mesh axis runs over, the one named last changes fastest.
Arguments:
- tile_data: bfloat16 [10240, 128, 128], P(('wide', 'narrow')), may hold values from -0.119628906 to 0.119628906
- tile_user: int32 [10240], P(('wide', 'narrow')), may hold values from 0 to 15
- tile_item: int32 [10240], P(('wide', 'narrow')), may hold values from 0 to 7
- tile_word: int32 [10240], P(('wide', 'narrow')), may hold values from 0 to 4095
- tile_month: int32 [10240], P(('wide', 'narrow')), may hold values from 0 to 999
- tile_live: int32 [32], P(('wide', 'narrow')), may hold values from 160 to 320, as said below
- user_need: int32 [32, 16], P(('wide', 'narrow')), may hold values from 0 to 127, as said below
- item_need: int32 [32, 8], P(('wide', 'narrow')), may hold values from 0 to 127, as said below
- user_slot: int32 [128], replicated, may hold values from 0 to 127, as said below
- item_slot: int32 [128], replicated, may hold values from 0 to 127, as said below
- user_factor: bfloat16 [16384, 128], P('wide'), may hold values from -6 to 6
- word_factor: bfloat16 [4096, 128], replicated, may hold values from -6 to 6
- month_factor: bfloat16 [1000, 128], replicated, may hold values from -6 to 6
Outputs:
- item_rows: float32 [16384, 128], P(('wide', 'narrow'))
The draws below stay inside these ranges and needn't reach their ends.
Inputs may be any that keep to these rules, and one draw needn't show every extreme that they name: user_slot is a permutation; the owner of user block b is user_slot[b] // 16. item_slot is a permutation; the owner of item block b is item_slot[b] // 16. `user_need`: entries k * 2 to k * 2 + 1 of each row are distinct user blocks whose owner is k. `item_need`: entry k of each row is an item block whose owner is k. `tile_live`: some device has all its slots live.
All inputs are finite; a program needn't handle non-finite values.
Results may differ from the reference program's by a relative error of at most 0.0029.
Values may be sent and summed in bfloat16 or wider, within the bound.
No kernel may reach another device: no remote copies, remote signals or barrier semaphores. Data moves between devices by JAX's collectives and lax.ppermute only.
A program may use at most 128 MiB of HBM per device.

```python
import jax
import jax.numpy as jnp
from jax import lax

R = 128
BS = 128
WORDS = 4096
MONTHS = 1000
TILES_DEV = 320
UB_OWN = 16
IB_OWN = 16
UPO = 2
IPO = 1
NDEV = 32
TILES = 10240
NUB = 128
NIB = 128
N_WIDE = 8


def choose_owned(key, per_owner, owned, inverse):
    scores = jax.random.randint(key, (NDEV, N_WIDE, owned), 0, 1 << 20) * owned
    scores = scores + jnp.arange(owned, dtype=jnp.int32)[None, None, :]
    picked = jnp.argsort(scores, axis=-1)[:, :, :per_owner].astype(jnp.int32)
    position = picked + (jnp.arange(N_WIDE, dtype=jnp.int32) * owned)[None, :, None]
    return inverse[position].reshape(NDEV, N_WIDE * per_owner).astype(jnp.int32)


def layout_tables(key):
    base = jax.random.fold_in(key, 9173)
    keys = jax.random.split(base, 8)
    user_slot = jax.random.permutation(keys[0], NUB).astype(jnp.int32)
    item_slot = jax.random.permutation(keys[1], NIB).astype(jnp.int32)
    user_inverse = jnp.argsort(user_slot).astype(jnp.int32)
    item_inverse = jnp.argsort(item_slot).astype(jnp.int32)
    user_need = choose_owned(keys[2], UPO, UB_OWN, user_inverse)
    item_need = choose_owned(keys[3], IPO, IB_OWN, item_inverse)
    tile_user = jax.random.randint(keys[4], (NDEV * TILES_DEV,), 0, N_WIDE * UPO).astype(jnp.int32)
    tile_item = jax.random.randint(keys[5], (NDEV * TILES_DEV,), 0, N_WIDE * IPO).astype(jnp.int32)
    tile_live = jax.random.randint(keys[6], (NDEV,), TILES_DEV // 2, TILES_DEV + 1).astype(jnp.int32)
    fullest = jax.random.randint(keys[7], (), 0, NDEV)
    tile_live = tile_live.at[fullest].set(TILES_DEV)
    return (user_slot, item_slot, user_need, item_need, tile_user, tile_item, tile_live)


def draw_user_slot(key, part):
    return layout_tables(key)[0]


def draw_item_slot(key, part):
    return layout_tables(key)[1]


def draw_user_need(key, part):
    return layout_tables(key)[2]


def draw_item_need(key, part):
    return layout_tables(key)[3]


def draw_tile_user(key, part):
    return layout_tables(key)[4]


def draw_tile_item(key, part):
    return layout_tables(key)[5]


def draw_tile_live(key, part):
    return layout_tables(key)[6]


def place_ends(values, rng, least, largest):
    dims = values.shape
    spot = [jax.random.randint(jax.random.fold_in(rng, axis), (), 0, dims[axis]) for axis in range(len(dims))]
    values = values.at[tuple(spot)].set(least)
    longest = dims.index(max(dims))
    spot[longest] = (spot[longest] + 1) % dims[longest]
    return values.at[tuple(spot)].set(largest)


def block_levels(stream_key, dims, cuts, least, largest):
    gain, own = 1.0, jax.random.fold_in(stream_key, 6)
    for dim, parts in cuts:
        heights = jnp.exp(jax.random.uniform(jax.random.fold_in(own, dim), (parts,), jnp.float32, least / len(cuts), largest / len(cuts)))
        gain = gain * jnp.repeat(heights, dims[dim] // parts).reshape([-1 if axis == dim else 1 for axis in range(len(dims))])
    return gain


def gaussian(key, extent, width, reach, cuts=(), held_as=jnp.bfloat16):
    gain = block_levels(key, extent, cuts, -0.22, 0.18) if cuts else 1.0
    result = jax.random.normal(key, extent, jnp.float32) * width * gain
    return jnp.minimum(jnp.maximum(result, -reach), reach).astype(held_as)


def setup_inputs(seed: int = 0) -> dict:
    splits = jax.random.split(jax.random.key(seed), 14)
    return {
        "tile_data": gaussian(splits[0], (TILES, BS, BS), 0.02, 0.119628906, ((0, 32),)),
        "tile_user": draw_tile_user(jax.random.fold_in(splits[13], 71), 0),
        "tile_item": draw_tile_item(jax.random.fold_in(splits[13], 71), 0),
        "tile_word": place_ends(jax.random.randint(splits[3], (TILES,), 0, WORDS), jax.random.fold_in(splits[3], 1), 0, WORDS - 1).astype(jnp.int32),
        "tile_month": place_ends(jax.random.randint(splits[4], (TILES,), 0, MONTHS), jax.random.fold_in(splits[4], 1), 0, MONTHS - 1).astype(jnp.int32),
        "tile_live": draw_tile_live(jax.random.fold_in(splits[13], 71), 0),
        "user_need": draw_user_need(jax.random.fold_in(splits[13], 71), 0),
        "item_need": draw_item_need(jax.random.fold_in(splits[13], 71), 0),
        "user_slot": draw_user_slot(jax.random.fold_in(splits[13], 71), 0),
        "item_slot": draw_item_slot(jax.random.fold_in(splits[13], 71), 0),
        "user_factor": gaussian(splits[10], (NUB * BS, R), 1.0, 6.0, ((0, 8),)),
        "word_factor": gaussian(splits[11], (WORDS, R), 1.0, 6.0),
        "month_factor": gaussian(splits[12], (MONTHS, R), 1.0, 6.0),
    }


def reference(tile_data, tile_user, tile_item, tile_word, tile_month, tile_live, user_need, item_need, user_slot, item_slot, user_factor, word_factor, month_factor):
    user_block = jnp.take_along_axis(user_need, tile_user.reshape(NDEV, TILES_DEV), axis=1)
    user_stored = user_slot[user_block].astype(jnp.int32)
    item_block = jnp.take_along_axis(item_need, tile_item.reshape(NDEV, TILES_DEV), axis=1)
    item_stored = item_slot[item_block].astype(jnp.int32)
    live_mask = (lax.iota(jnp.int32, TILES_DEV)[None, :] < tile_live[:, None]).astype(jnp.float32)
    factor_blocks = user_factor.reshape(NUB, BS, R)
    word_month = word_factor[tile_word].astype(jnp.float32) * month_factor[tile_month].astype(jnp.float32)
    word_month = word_month.reshape(NDEV, TILES_DEV, R)

    def one_device(total, packed):
        data, stored, target, factor_scale, mask = packed
        scaled = (factor_blocks[stored].astype(jnp.float32) * factor_scale[:, None, :]).astype(jnp.bfloat16)
        contrib = jnp.einsum("tab,tar->tbr", data.astype(jnp.float32), scaled.astype(jnp.float32))
        contrib = contrib * mask[:, None, None]
        return total.at[target].add(contrib), None

    start = jnp.zeros((NIB, BS, R), jnp.float32)
    total, _ = lax.scan(one_device, start, (tile_data.reshape(NDEV, TILES_DEV, BS, BS), user_stored, item_stored, word_month, live_mask))
    return total.reshape(NIB * BS, R)
```

```python
import functools

import jax
import jax.numpy as jnp
from jax import lax
from jax.experimental import pallas as pl
from jax.experimental.pallas import tpu as pltpu
from jax.sharding import PartitionSpec as P

GROUP = 4
CHUNKS = 4
SMEM = pl.BlockSpec(memory_space=pltpu.SMEM)
VMEM = pl.BlockSpec(memory_space=pltpu.VMEM)


def sort_kernel(live, user, item, scale, order, users, chunk_item, steps, scale_sorted, place):
    touched = place.shape[0]
    slots = order.shape[0]
    scale_sorted[...] = jnp.zeros_like(scale_sorted)

    def clear(q, _):
        place[q] = 0
        return 0

    lax.fori_loop(0, touched, clear, 0)

    def blank(p, _):
        order[p] = 0
        users[p] = 0
        return 0

    lax.fori_loop(0, slots, blank, 0, unroll=8)

    def blank_item(p, _):
        chunk_item[p] = 0
        return 0

    lax.fori_loop(0, slots // GROUP, blank_item, 0, unroll=8)
    count = live[0]

    def tally(t, _):
        q = item[t]
        place[q] = place[q] + 1
        return 0

    lax.fori_loop(0, count, tally, 0)

    def offset(q, chunk):
        n = (place[q] + GROUP - 1) // GROUP
        place[q] = chunk * GROUP

        def mark(c, _):
            chunk_item[chunk + c] = q
            return 0

        lax.fori_loop(0, n, mark, 0)
        return chunk + n

    chunks = lax.fori_loop(0, touched, offset, 0)
    steps[0] = (chunks + CHUNKS - 1) // CHUNKS

    def put(t, _):
        q = item[t]
        p = place[q]
        place[q] = p + 1
        order[p] = t
        users[p] = user[t]
        scale_sorted[pl.ds(p, 1), :] = scale[pl.ds(t, 1), :]
        return 0

    lax.fori_loop(0, count, put, 0)


def sort_tiles(live, user, item, scale, touched):
    tiles, width = scale.shape
    per_step = GROUP * CHUNKS
    slots = -(-(tiles + touched * (GROUP - 1)) // per_step) * per_step
    ints = lambda n: jax.ShapeDtypeStruct((n,), jnp.int32)
    return pl.pallas_call(
        sort_kernel,
        out_shape=(
            ints(slots),
            ints(slots),
            ints(slots // GROUP),
            ints(1),
            jax.ShapeDtypeStruct((slots, width), jnp.float32),
        ),
        in_specs=[SMEM, SMEM, SMEM, VMEM],
        out_specs=(SMEM, SMEM, SMEM, SMEM, VMEM),
        scratch_shapes=[pltpu.SMEM((touched,), jnp.int32)],
        compiler_params=pltpu.CompilerParams(vmem_limit_bytes=4 << 20),
        cost_estimate=pl.CostEstimate(flops=1 << 20, bytes_accessed=4 << 20, transcendentals=0),
        name="sort_tiles",
    )(live, user, item, scale)


def answer_kernel(owned, asked, slot, blocks, out):
    wide, per = asked.shape

    def give(k, _):
        for j in range(per):
            out[k * per + j] = blocks[lax.rem(slot[asked[k, j]], owned)]
        return 0

    lax.fori_loop(0, wide, give, 0)


def answer(asked, slot, blocks):
    wide, per = asked.shape
    owned, side, width = blocks.shape
    return pl.pallas_call(
        functools.partial(answer_kernel, owned),
        out_shape=jax.ShapeDtypeStruct((wide * per, side, width), blocks.dtype),
        in_specs=[SMEM, SMEM, VMEM],
        out_specs=VMEM,
        name="answer",
    )(asked, slot, blocks)


def contract_kernel(order, users, chunk_item, steps, tiles, blocks, scale, out, turned, total):
    def turn(u, _):
        turned[u] = blocks[u].astype(jnp.float32).T
        return 0

    lax.fori_loop(0, blocks.shape[0], turn, 0)
    total[...] = jnp.zeros_like(total)
    per_step = GROUP * CHUNKS

    def step(i, _):
        first = pl.multiple_of(i * per_step, per_step)
        columns = scale[pl.ds(first, per_step), :].T
        for c in range(CHUNKS):
            left, right = [], []
            for g in range(GROUP):
                n = c * GROUP + g
                left.append((turned[users[first + n]] * columns[:, n : n + 1]).astype(jnp.bfloat16))
                right.append(tiles[order[first + n]])
            part = jnp.dot(
                jnp.concatenate(left, 1),
                jnp.concatenate(right, 0),
                preferred_element_type=jnp.float32,
            )
            q = chunk_item[i * CHUNKS + c]
            total[q] = total[q] + part
        return 0

    lax.fori_loop(0, steps[0], step, 0)

    def finish(q, _):
        out[q] = total[q].T.astype(out.dtype)
        return 0

    lax.fori_loop(0, out.shape[0], finish, 0)


def contract(order, users, chunk_item, steps, tiles, blocks, scale, touched):
    count, side, width = blocks.shape
    return pl.pallas_call(
        contract_kernel,
        out_shape=jax.ShapeDtypeStruct((touched, side, width), jnp.bfloat16),
        in_specs=[SMEM, SMEM, SMEM, SMEM, VMEM, VMEM, VMEM],
        out_specs=VMEM,
        scratch_shapes=[
            pltpu.VMEM((count, width, side), jnp.float32),
            pltpu.VMEM((touched, width, side), jnp.float32),
        ],
        compiler_params=pltpu.CompilerParams(vmem_limit_bytes=40 << 20),
        cost_estimate=pl.CostEstimate(
            flops=2 * tiles.shape[0] * side * side * width,
            bytes_accessed=2 * tiles.size,
            transcendentals=0,
        ),
        name="contract",
    )(order, users, chunk_item, steps, tiles, blocks, scale)


def merge_kernel(items_owned, me, came, slot, parts, mine, *rest):
    sends, total = rest[:-1], rest[-1]
    share = mine.shape[0]
    total[...] = jnp.zeros_like(total)

    def add(n, _):
        j = lax.rem(slot[came[n]], items_owned)
        total[j] = total[j] + parts[n].astype(jnp.float32)
        return 0

    lax.fori_loop(0, parts.shape[0], add, 0)
    for d in range(items_owned // share):
        first = (me[0] ^ d) * share
        for j in range(share):
            if d == 0:
                mine[j] = total[first + j]
            else:
                sends[d - 1][j] = total[first + j].astype(jnp.bfloat16)


def merge(me, came, slot, parts, items_owned, members):
    side, width = parts.shape[1:]
    share = items_owned // members
    piece = lambda kind: jax.ShapeDtypeStruct((share, side, width), kind)
    return pl.pallas_call(
        functools.partial(merge_kernel, items_owned),
        out_shape=(piece(jnp.float32),) + (piece(jnp.bfloat16),) * (members - 1),
        in_specs=[SMEM, SMEM, SMEM, VMEM],
        out_specs=(VMEM,) * members,
        scratch_shapes=[pltpu.VMEM((items_owned, side, width), jnp.float32)],
        name="merge",
    )(me, came, slot, parts)


def shards(
    tile_data,
    tile_user,
    tile_item,
    tile_word,
    tile_month,
    tile_live,
    user_need,
    item_need,
    user_slot,
    item_slot,
    user_factor,
    word_factor,
    month_factor,
):
    wide = lax.axis_size("wide")
    members = lax.axis_size("narrow")
    side = tile_data.shape[1]
    width = user_factor.shape[1]
    touched = item_need.shape[1]
    items_owned = item_slot.shape[0] // wide
    need = jnp.concatenate([user_need.reshape(wide, -1), item_need.reshape(wide, -1)], axis=1)
    heard = lax.all_to_all(need, "wide", split_axis=0, concat_axis=0, tiled=True)
    per_user = user_need.shape[1] // wide
    asked, came = heard[:, :per_user], heard[:, per_user:].reshape(-1)
    replies = answer(asked, user_slot, user_factor.reshape(-1, side, width))
    fetched = lax.all_to_all(
        replies.reshape(wide, per_user, side, width), "wide", split_axis=0, concat_axis=0, tiled=True
    ).reshape(-1, side, width)
    scale = word_factor[tile_word].astype(jnp.float32) * month_factor[tile_month].astype(jnp.float32)
    order, users, chunk_item, steps, scale_sorted = sort_tiles(
        tile_live, tile_user, tile_item, scale, touched
    )
    partial = contract(order, users, chunk_item, steps, tile_data, fetched, scale_sorted, touched)
    arrived = lax.all_to_all(
        partial.reshape(wide, -1, side, width), "wide", split_axis=0, concat_axis=0, tiled=True
    ).reshape(-1, side, width)
    me = lax.axis_index("narrow").reshape(1)
    pieces = merge(me, came, item_slot, arrived, items_owned, members)
    rows = pieces[0]
    for d in range(1, members):
        got = lax.ppermute(pieces[d], "narrow", [(n, n ^ d) for n in range(members)])
        rows = rows + got.astype(jnp.float32)
    return rows.reshape(-1, width)


def solution(mesh):
    return jax.shard_map(
        shards,
        mesh=mesh,
        in_specs=(
            P(("wide", "narrow"), None, None),
            P(("wide", "narrow")),
            P(("wide", "narrow")),
            P(("wide", "narrow")),
            P(("wide", "narrow")),
            P(("wide", "narrow")),
            P(("wide", "narrow"), None),
            P(("wide", "narrow"), None),
            P(),
            P(),
            P("wide", None),
            P(),
            P(),
        ),
        out_specs=P(("wide", "narrow"), None),
        check_vma=False,
    )
```

```python
import functools

import jax
import jax.numpy as jnp
from jax import lax
from jax.experimental import pallas as pl
from jax.experimental.pallas import tpu as pltpu
from jax.sharding import PartitionSpec as P

CONTRACT_MIB = 12
ANSWER_MIB = 12
RANK_MIB = 63
TURN_MIB = 12
TURN = 32
GROUP = 4
CHUNKS = 12
SMEM = pl.BlockSpec(memory_space=pltpu.SMEM)
VMEM = pl.BlockSpec(memory_space=pltpu.VMEM)
HBM = pl.BlockSpec(memory_space=pltpu.HBM)


def rank_kernel(
    per, pad_count, me, live, user, word, month, item, words, months,
    plan, scale,
    word_held, month_held, word_rows, month_rows, place_v, count_v, offset_v,
    place, count, offset, fetch,
):
    tile_count = item.shape[0]
    touched = count.shape[1]
    slots = scale.shape[0]
    dump = slots - 16
    tables = [
        pltpu.make_async_copy(words, word_held, fetch.at[3]),
        pltpu.make_async_copy(months, month_held, fetch.at[4]),
    ]
    for copy in tables:
        copy.start()
    rows = lax.broadcasted_iota(jnp.int32, (touched, tile_count), 0)
    lanes = lax.broadcasted_iota(jnp.int32, (touched, tile_count), 1)
    one = jnp.where((rows == item[...].reshape(1, tile_count)) & (lanes < live[0]), 1.0, 0.0)
    one_half = one.astype(jnp.bfloat16)
    before = jnp.where(
        lax.broadcasted_iota(jnp.int32, (tile_count, tile_count), 0)
        < lax.broadcasted_iota(jnp.int32, (tile_count, tile_count), 1),
        1.0,
        0.0,
    ).astype(jnp.bfloat16)
    rank = jnp.dot(one_half, before, preferred_element_type=jnp.float32)
    small_rows = lax.broadcasted_iota(jnp.int32, (touched, touched), 0)
    small_lanes = lax.broadcasted_iota(jnp.int32, (touched, touched), 1)
    chunks_of = lambda n: jnp.floor((n + (GROUP - 1)) * (1.0 / GROUP))
    count_column = jnp.sum(one, axis=1, keepdims=True)
    chunks_column = jnp.broadcast_to(chunks_of(count_column), (touched, 128)).astype(jnp.bfloat16)
    offset_column = GROUP * jnp.dot(
        jnp.where(small_lanes < small_rows, 1.0, 0.0).astype(jnp.bfloat16),
        chunks_column,
        preferred_element_type=jnp.float32,
    )[:, :1]
    here = jnp.sum(one * (rank + offset_column), axis=0, keepdims=True)
    lane = lax.broadcasted_iota(jnp.int32, (1, tile_count), 1)
    place_v[...] = jnp.where(lane < live[0], here.astype(jnp.int32), dump + lax.rem(lane, 16))
    count_row = lax.dot_general(
        jnp.ones((8, tile_count), jnp.bfloat16),
        one_half,
        (((1,), (1,)), ((), ())),
        preferred_element_type=jnp.float32,
    )
    offset_row = GROUP * jnp.dot(
        chunks_of(count_row).astype(jnp.bfloat16),
        jnp.where(small_rows < small_lanes, 1.0, 0.0).astype(jnp.bfloat16),
        preferred_element_type=jnp.float32,
    )
    count_v[...] = count_row.astype(jnp.int32)
    offset_v[...] = offset_row.astype(jnp.int32)
    fetched = [
        pltpu.make_async_copy(source, sink, fetch.at[n])
        for n, (source, sink) in enumerate(((place_v, place), (count_v, count), (offset_v, offset)))
    ]
    for copy in fetched:
        copy.start()
    for copy in tables:
        copy.wait()
    word_rows[...] = word_held[...].astype(jnp.float32)
    month_rows[...] = month_held[...].astype(jnp.float32)
    for copy in fetched:
        copy.wait()
    places = slots + slots // GROUP + 1
    pads = places + tile_count
    for n in range(pad_count):
        plan[pads + n] = dump + n % 16
    nothing = jnp.zeros((1, scale.shape[1]), scale.dtype)

    def blank(n, p):
        plan[pads + n] = p
        plan[p] = 0
        scale[pl.ds(p, 1), :] = nothing

    def pad(q, blanks):
        first, n = offset[0, q], count[0, q]
        chunks = (n + GROUP - 1) // GROUP

        def mark(c, _):
            plan[slots + first // GROUP + c] = q
            return 0

        def fill(p, blanks):
            blank(blanks, p)
            return blanks + 1

        lax.fori_loop(0, chunks, mark, 0)
        return lax.fori_loop(first + n, first + chunks * GROUP, fill, blanks)

    blanks = lax.fori_loop(0, touched, pad, 0)
    last = offset[0, touched - 1] // GROUP
    chunks = last + (count[0, touched - 1] + GROUP - 1) // GROUP
    for c in range(CHUNKS - 1):
        plan[slots + chunks + c] = 0
        for g in range(GROUP):
            blank(blanks + c * GROUP + g, (chunks + c) * GROUP + g)
    plan[places - 1] = (chunks + CHUNKS - 1) // CHUNKS

    def put(c, _):
        for n in range(16):
            t = c * 16 + n
            p = place[0, t]
            scale[pl.ds(p, 1), :] = (
                word_rows[pl.ds(word[t], 1), :] * month_rows[pl.ds(month[t], 1), :]
            )
            u = user[t]
            plan[p] = (lax.div(u, per) ^ me[0]) * per + lax.rem(u, per)
            plan[places + t] = p
        return 0

    lax.fori_loop(0, tile_count // 16, put, 0)


def slots_for(tile_count, touched):
    per_step = GROUP * CHUNKS
    return -(-(tile_count + touched * (GROUP - 1)) // per_step) * per_step + per_step + 16


def rank(me, per, live, user, item, word, month, words, months, touched):
    tile_count = user.shape[0]
    width = words.shape[1]
    slots = slots_for(tile_count, touched)
    pads = touched * (GROUP - 1) + (CHUNKS - 1) * GROUP
    shape = jax.ShapeDtypeStruct
    return pl.pallas_call(
        functools.partial(rank_kernel, per, pads),
        out_shape=(
            shape((slots + slots // GROUP + 1 + tile_count + pads,), jnp.int32),
            shape((slots, width), jnp.float32),
        ),
        in_specs=[SMEM] * 5 + [VMEM, HBM, HBM],
        out_specs=(SMEM, VMEM),
        scratch_shapes=[
            pltpu.VMEM(words.shape, words.dtype),
            pltpu.VMEM(months.shape, months.dtype),
            pltpu.VMEM(words.shape, jnp.float32),
            pltpu.VMEM(months.shape, jnp.float32),
            pltpu.VMEM((1, tile_count), jnp.int32),
            pltpu.VMEM((8, touched), jnp.int32),
            pltpu.VMEM((8, touched), jnp.int32),
            pltpu.SMEM((1, tile_count), jnp.int32),
            pltpu.SMEM((8, touched), jnp.int32),
            pltpu.SMEM((8, touched), jnp.int32),
            pltpu.SemaphoreType.DMA((5,)),
        ],
        compiler_params=pltpu.CompilerParams(vmem_limit_bytes=RANK_MIB << 20),
        cost_estimate=pl.CostEstimate(flops=1 << 33, bytes_accessed=1 << 25, transcendentals=0),
        name="rank",
    )(me, live, user, word, month, item, words, months)


def turn_kernel(pad_count, plan, tiles, turned):
    tile_count = tiles.shape[0]
    slots = turned.shape[0]
    places = slots + slots // GROUP + 1
    nothing = jnp.zeros(turned.shape[1:], turned.dtype)

    def clear(n, _):
        turned[plan[places + tile_count + n]] = nothing
        return 0

    lax.fori_loop(0, pad_count, clear, 0, unroll=4)

    def put(c, _):
        for n in range(TURN):
            t = c * TURN + n
            turned[plan[places + t]] = tiles[t].T
        return 0

    lax.fori_loop(0, tile_count // TURN, put, 0)


def turn(plan, tiles, slots):
    tile_count, side = tiles.shape[:2]
    pads = plan.shape[0] - (slots + slots // GROUP + 1 + tile_count)
    return pl.pallas_call(
        functools.partial(turn_kernel, pads),
        out_shape=jax.ShapeDtypeStruct((slots, side, side), tiles.dtype),
        in_specs=[SMEM, VMEM],
        out_specs=VMEM,
        compiler_params=pltpu.CompilerParams(vmem_limit_bytes=TURN_MIB << 20),
        cost_estimate=pl.CostEstimate(
            flops=1 << 30, bytes_accessed=4 * tiles.size, transcendentals=0
        ),
        name="turn",
    )(plan, tiles)


def ask_kernel(user_need, item_need, need):
    wide = need.shape[0]
    per_user, per_item = user_need.shape[1] // wide, item_need.shape[1] // wide
    for k in range(wide):
        for j in range(per_user):
            need[k, 0, j] = user_need[0, k * per_user + j]
        for j in range(per_item):
            need[k, 0, per_user + j] = item_need[0, k * per_item + j]


def ask(user_need, item_need, wide):
    per = (user_need.shape[1] + item_need.shape[1]) // wide
    return pl.pallas_call(
        ask_kernel,
        out_shape=jax.ShapeDtypeStruct((wide, 1, per), jnp.int32),
        in_specs=[SMEM, SMEM],
        out_specs=SMEM,
        compiler_params=pltpu.CompilerParams(vmem_limit_bytes=63 << 20),
        name="ask",
    )(user_need, item_need)


def answer_kernel(owned, per, me, heard, slot, blocks, *outs):
    for d, out in enumerate(outs):
        k = me[0] ^ d
        for j in range(per):
            out[j] = blocks[lax.rem(slot[heard[k, 0, j]], owned)]


def answer(me, heard, slot, blocks, per):
    owned, side, width = blocks.shape
    wide = heard.shape[0]
    return pl.pallas_call(
        functools.partial(answer_kernel, owned, per),
        out_shape=(jax.ShapeDtypeStruct((per, side, width), blocks.dtype),) * wide,
        in_specs=[SMEM, SMEM, SMEM, VMEM],
        out_specs=(VMEM,) * wide,
        compiler_params=pltpu.CompilerParams(vmem_limit_bytes=ANSWER_MIB << 20),
        cost_estimate=pl.CostEstimate(flops=1 << 33, bytes_accessed=1 << 25, transcendentals=0),
        name="answer",
    )(me, heard, slot, blocks)


def contract_kernel(plan, scale, turned, *refs):
    fetched, (out, wide_blocks, total) = refs[:-3], refs[-3:]
    per = fetched[0].shape[0]
    slots = scale.shape[0]
    per_step = GROUP * CHUNKS
    for d, blocks in enumerate(fetched):
        for j in range(per):
            wide_blocks[d * per + j] = blocks[j].astype(jnp.float32)
    total[...] = jnp.zeros_like(total)

    def step(i, _):
        first = i * per_step
        for c in range(CHUNKS):
            left, right = [], []
            for g in range(GROUP):
                p = first + c * GROUP + g
                left.append(turned[p])
                right.append((wide_blocks[plan[p]] * scale[pl.ds(p, 1), :]).astype(jnp.bfloat16))
            part = jnp.dot(
                jnp.concatenate(left, 1),
                jnp.concatenate(right, 0),
                preferred_element_type=jnp.float32,
            )
            q = plan[slots + i * CHUNKS + c]
            total[q] = total[q] + part
        return 0

    lax.fori_loop(0, plan[slots + slots // GROUP], step, 0)
    out[...] = total[...].astype(out.dtype)


def contract(plan, scale, turned, fetched, touched):
    per, side, width = fetched[0].shape
    return pl.pallas_call(
        contract_kernel,
        out_shape=jax.ShapeDtypeStruct((touched, side, width), jnp.bfloat16),
        in_specs=[SMEM, VMEM, VMEM] + [VMEM] * len(fetched),
        out_specs=VMEM,
        scratch_shapes=[
            pltpu.VMEM((len(fetched) * per, side, width), jnp.float32),
            pltpu.VMEM((touched, side, width), jnp.float32),
        ],
        compiler_params=pltpu.CompilerParams(vmem_limit_bytes=CONTRACT_MIB << 20),
        cost_estimate=pl.CostEstimate(
            flops=2 * turned.size * width, bytes_accessed=turned.size, transcendentals=0
        ),
        name="contract",
    )(plan, scale, turned, *fetched)


def merge_kernel(items_owned, per, me, heard, slot, parts, mine, *rest):
    sends, total = rest[:-1], rest[-1]
    share = mine.shape[0]
    total[...] = jnp.zeros_like(total)

    base = heard.shape[2] - per

    def add(k, _):
        for n in range(per):
            j = lax.rem(slot[heard[k, 0, base + n]], items_owned)
            total[j] = total[j] + parts[k * per + n].astype(jnp.float32)
        return 0

    lax.fori_loop(0, heard.shape[0], add, 0)
    for d in range(items_owned // share):
        first = (me[0] ^ d) * share
        for j in range(share):
            if d == 0:
                mine[j] = total[first + j]
            else:
                sends[d - 1][j] = total[first + j].astype(jnp.bfloat16)


def merge(me, heard, slot, parts, items_owned, members, per):
    side, width = parts.shape[1:]
    share = items_owned // members
    piece = lambda kind: jax.ShapeDtypeStruct((share, side, width), kind)
    return pl.pallas_call(
        functools.partial(merge_kernel, items_owned, per),
        out_shape=(piece(jnp.float32),) + (piece(jnp.bfloat16),) * (members - 1),
        in_specs=[SMEM, SMEM, SMEM, VMEM],
        out_specs=(VMEM,) * members,
        scratch_shapes=[pltpu.VMEM((items_owned, side, width), jnp.float32)],
        compiler_params=pltpu.CompilerParams(vmem_limit_bytes=12 << 20),
        name="merge",
    )(me, heard, slot, parts)


def body(
    tile_data,
    tile_user,
    tile_item,
    tile_word,
    tile_month,
    tile_live,
    user_need,
    item_need,
    user_slot,
    item_slot,
    user_factor,
    word_factor,
    month_factor,
):
    wide = lax.axis_size("wide")
    members = lax.axis_size("narrow")
    side = tile_data.shape[1]
    width = user_factor.shape[1]
    touched = item_need.shape[1]
    items_owned = item_slot.shape[0] // wide
    per_user = user_need.shape[1] // wide
    heard = lax.all_to_all(
        ask(user_need, item_need, wide), "wide", split_axis=0, concat_axis=0, tiled=True
    )
    me_wide = lax.axis_index("wide").reshape(1)
    plan, scale = rank(
        me_wide,
        per_user,
        tile_live,
        tile_user,
        tile_item,
        tile_word,
        tile_month,
        word_factor,
        month_factor,
        touched,
    )
    replies = answer(me_wide, heard, user_slot, user_factor.reshape(-1, side, width), per_user)
    fetched = list(replies)
    for d in reversed(range(1, wide)):
        fetched[d] = lax.ppermute(replies[d], "wide", [(k, k ^ d) for k in range(wide)])
    turned = turn(plan, tile_data, scale.shape[0])
    partial = contract(plan, scale, turned, fetched, touched)
    arrived = lax.all_to_all(
        partial.reshape(wide, -1, side, width), "wide", split_axis=0, concat_axis=0, tiled=True
    ).reshape(-1, side, width)
    me = lax.axis_index("narrow").reshape(1)
    pieces = merge(me, heard, item_slot, arrived, items_owned, members, touched // wide)
    rows = pieces[0]
    for d in range(1, members):
        got = lax.ppermute(pieces[d], "narrow", [(n, n ^ d) for n in range(members)])
        rows = rows + got.astype(jnp.float32)
    return rows.reshape(-1, width)


def solution(mesh):
    return jax.shard_map(
        body,
        mesh=mesh,
        in_specs=(
            P(("wide", "narrow"), None, None),
            P(("wide", "narrow")),
            P(("wide", "narrow")),
            P(("wide", "narrow")),
            P(("wide", "narrow")),
            P(("wide", "narrow")),
            P(("wide", "narrow"), None),
            P(("wide", "narrow"), None),
            P(),
            P(),
            P("wide", None),
            P(),
            P(),
        ),
        out_specs=P(("wide", "narrow"), None),
        check_vma=False,
    )
```

```python
import functools

import jax
import jax.numpy as jnp
from jax import lax
from jax.experimental import pallas as pl
from jax.experimental.pallas import tpu as pltpu
from jax.sharding import PartitionSpec as P

CONTRACT_MIB = 12
ANSWER_MIB = 12
RANK_MIB = 63
TURN_MIB = 12
TURN = 32
GROUP = 4
CHUNKS = 12
SMEM = pl.BlockSpec(memory_space=pltpu.SMEM)
VMEM = pl.BlockSpec(memory_space=pltpu.VMEM)
HBM = pl.BlockSpec(memory_space=pltpu.HBM)


def rank_kernel(
    slots, pad_count, me, live, user, item, plan, place_v, count_v, offset_v, place, count, offset, fetch
):
    tile_count = item.shape[0]
    touched = count.shape[1]
    dump = slots - 16
    rows = lax.broadcasted_iota(jnp.int32, (touched, tile_count), 0)
    lanes = lax.broadcasted_iota(jnp.int32, (touched, tile_count), 1)
    one = jnp.where((rows == item[...].reshape(1, tile_count)) & (lanes < live[0]), 1.0, 0.0)
    one_half = one.astype(jnp.bfloat16)
    before = jnp.where(
        lax.broadcasted_iota(jnp.int32, (tile_count, tile_count), 0)
        < lax.broadcasted_iota(jnp.int32, (tile_count, tile_count), 1),
        1.0,
        0.0,
    ).astype(jnp.bfloat16)
    rank = jnp.dot(one_half, before, preferred_element_type=jnp.float32)
    small_rows = lax.broadcasted_iota(jnp.int32, (touched, touched), 0)
    small_lanes = lax.broadcasted_iota(jnp.int32, (touched, touched), 1)
    chunks_of = lambda n: jnp.floor((n + (GROUP - 1)) * (1.0 / GROUP))
    count_column = jnp.sum(one, axis=1, keepdims=True)
    chunks_column = jnp.broadcast_to(chunks_of(count_column), (touched, 128)).astype(jnp.bfloat16)
    offset_column = GROUP * jnp.dot(
        jnp.where(small_lanes < small_rows, 1.0, 0.0).astype(jnp.bfloat16),
        chunks_column,
        preferred_element_type=jnp.float32,
    )[:, :1]
    here = jnp.sum(one * (rank + offset_column), axis=0, keepdims=True)
    lane = lax.broadcasted_iota(jnp.int32, (1, tile_count), 1)
    place_v[...] = jnp.where(lane < live[0], here.astype(jnp.int32), dump + lax.rem(lane, 16))
    count_row = lax.dot_general(
        jnp.ones((8, tile_count), jnp.bfloat16),
        one_half,
        (((1,), (1,)), ((), ())),
        preferred_element_type=jnp.float32,
    )
    offset_row = GROUP * jnp.dot(
        chunks_of(count_row).astype(jnp.bfloat16),
        jnp.where(small_rows < small_lanes, 1.0, 0.0).astype(jnp.bfloat16),
        preferred_element_type=jnp.float32,
    )
    count_v[...] = count_row.astype(jnp.int32)
    offset_v[...] = offset_row.astype(jnp.int32)
    fetched = [
        pltpu.make_async_copy(source, sink, fetch.at[n])
        for n, (source, sink) in enumerate(((place_v, place), (count_v, count), (offset_v, offset)))
    ]
    for copy in fetched:
        copy.start()
    for copy in fetched:
        copy.wait()
    places = slots + slots // GROUP + 1
    pads = places + tile_count
    for n in range(pad_count):
        plan[pads + n] = dump + n % 16
    plan[plan.shape[0] - 1] = me[0]

    def blank(n, p):
        plan[pads + n] = p
        plan[p] = 0

    def pad(q, blanks):
        first, n = offset[0, q], count[0, q]
        chunks = (n + GROUP - 1) // GROUP

        def mark(c, _):
            plan[slots + first // GROUP + c] = q
            return 0

        def fill(p, blanks):
            blank(blanks, p)
            return blanks + 1

        lax.fori_loop(0, chunks, mark, 0)
        return lax.fori_loop(first + n, first + chunks * GROUP, fill, blanks)

    blanks = lax.fori_loop(0, touched, pad, 0)
    last = offset[0, touched - 1] // GROUP
    chunks = last + (count[0, touched - 1] + GROUP - 1) // GROUP
    for c in range(CHUNKS - 1):
        plan[slots + chunks + c] = 0
        for g in range(GROUP):
            blank(blanks + c * GROUP + g, (chunks + c) * GROUP + g)
    plan[places - 1] = (chunks + CHUNKS - 1) // CHUNKS

    def put(c, _):
        for n in range(TURN):
            t = c * TURN + n
            p = place[0, t]
            plan[p] = user[t]
            plan[places + t] = p
        return 0

    lax.fori_loop(0, tile_count // TURN, put, 0)


def slots_for(tile_count, touched):
    per_step = GROUP * CHUNKS
    return -(-(tile_count + touched * (GROUP - 1)) // per_step) * per_step + per_step + 16


def rank(me, live, user, item, touched):
    tile_count = user.shape[0]
    slots = slots_for(tile_count, touched)
    pads = touched * (GROUP - 1) + (CHUNKS - 1) * GROUP
    return pl.pallas_call(
        functools.partial(rank_kernel, slots, pads),
        out_shape=jax.ShapeDtypeStruct(
            (slots + slots // GROUP + 1 + tile_count + pads + 1,), jnp.int32
        ),
        in_specs=[SMEM, SMEM, SMEM, VMEM],
        out_specs=SMEM,
        scratch_shapes=[
            pltpu.VMEM((1, tile_count), jnp.int32),
            pltpu.VMEM((8, touched), jnp.int32),
            pltpu.VMEM((8, touched), jnp.int32),
            pltpu.SMEM((1, tile_count), jnp.int32),
            pltpu.SMEM((8, touched), jnp.int32),
            pltpu.SMEM((8, touched), jnp.int32),
            pltpu.SemaphoreType.DMA((3,)),
        ],
        compiler_params=pltpu.CompilerParams(vmem_limit_bytes=RANK_MIB << 20),
        cost_estimate=pl.CostEstimate(flops=1 << 33, bytes_accessed=1 << 25, transcendentals=0),
        name="rank",
    )(me, live, user, item)


def turn_kernel(
    pad_count, plan, word, month, tiles, words, months, turned, scale, word_rows, month_rows
):
    tile_count = tiles.shape[0]
    slots = turned.shape[0]
    places = slots + slots // GROUP + 1
    word_rows[...] = words[...].astype(jnp.float32)
    month_rows[...] = months[...].astype(jnp.float32)
    nothing = jnp.zeros(turned.shape[1:], turned.dtype)
    no_scale = jnp.zeros((1, scale.shape[1]), scale.dtype)

    def clear(n, _):
        p = plan[places + tile_count + n]
        turned[p] = nothing
        scale[pl.ds(p, 1), :] = no_scale
        return 0

    lax.fori_loop(0, pad_count, clear, 0, unroll=4)

    def put(c, _):
        for n in range(TURN):
            t = c * TURN + n
            p = plan[places + t]
            turned[p] = tiles[t].T
            scale[pl.ds(p, 1), :] = (
                word_rows[pl.ds(word[t], 1), :] * month_rows[pl.ds(month[t], 1), :]
            )
        return 0

    lax.fori_loop(0, tile_count // TURN, put, 0)


def turn(plan, word, month, tiles, words, months, slots):
    tile_count, side = tiles.shape[:2]
    width = words.shape[1]
    pads = plan.shape[0] - (slots + slots // GROUP + 1 + tile_count) - 1
    return pl.pallas_call(
        functools.partial(turn_kernel, pads),
        out_shape=(
            jax.ShapeDtypeStruct((slots, side, side), tiles.dtype),
            jax.ShapeDtypeStruct((slots, width), jnp.float32),
        ),
        in_specs=[SMEM, SMEM, SMEM, VMEM, VMEM, VMEM],
        out_specs=(VMEM, VMEM),
        scratch_shapes=[
            pltpu.VMEM(words.shape, jnp.float32),
            pltpu.VMEM(months.shape, jnp.float32),
        ],
        compiler_params=pltpu.CompilerParams(vmem_limit_bytes=TURN_MIB << 20),
        cost_estimate=pl.CostEstimate(
            flops=1 << 30, bytes_accessed=4 * tiles.size, transcendentals=0
        ),
        name="turn",
    )(plan, word, month, tiles, words, months)


def ask_kernel(user_need, item_need, need):
    wide = need.shape[0]
    per_user, per_item = user_need.shape[1] // wide, item_need.shape[1] // wide
    for k in range(wide):
        for j in range(per_user):
            need[k, 0, j] = user_need[0, k * per_user + j]
        for j in range(per_item):
            need[k, 0, per_user + j] = item_need[0, k * per_item + j]


def ask(user_need, item_need, wide):
    per = (user_need.shape[1] + item_need.shape[1]) // wide
    return pl.pallas_call(
        ask_kernel,
        out_shape=jax.ShapeDtypeStruct((wide, 1, per), jnp.int32),
        in_specs=[SMEM, SMEM],
        out_specs=SMEM,
        compiler_params=pltpu.CompilerParams(vmem_limit_bytes=63 << 20),
        name="ask",
    )(user_need, item_need)


def answer_kernel(owned, per, me, heard, slot, blocks, *outs):
    for d, out in enumerate(outs):
        k = me[0] ^ d
        for j in range(per):
            out[j] = blocks[lax.rem(slot[heard[k, 0, j]], owned)]


def answer(me, heard, slot, blocks, per):
    owned, side, width = blocks.shape
    wide = heard.shape[0]
    return pl.pallas_call(
        functools.partial(answer_kernel, owned, per),
        out_shape=(jax.ShapeDtypeStruct((per, side, width), blocks.dtype),) * wide,
        in_specs=[SMEM, SMEM, SMEM, VMEM],
        out_specs=(VMEM,) * wide,
        compiler_params=pltpu.CompilerParams(vmem_limit_bytes=ANSWER_MIB << 20),
        cost_estimate=pl.CostEstimate(flops=1 << 33, bytes_accessed=1 << 25, transcendentals=0),
        name="answer",
    )(me, heard, slot, blocks)


def contract_kernel(plan, scale, turned, *refs):
    fetched, (out, wide_blocks, total) = refs[:-3], refs[-3:]
    per = fetched[0].shape[0]
    slots = scale.shape[0]
    per_step = GROUP * CHUNKS
    me = plan[plan.shape[0] - 1]
    for d, blocks in enumerate(fetched):
        for j in range(per):
            wide_blocks[(me ^ d) * per + j] = blocks[j].astype(jnp.float32)
    total[...] = jnp.zeros_like(total)

    def step(i, _):
        first = i * per_step
        for c in range(CHUNKS):
            left, right = [], []
            for g in range(GROUP):
                p = first + c * GROUP + g
                left.append(turned[p])
                right.append((wide_blocks[plan[p]] * scale[pl.ds(p, 1), :]).astype(jnp.bfloat16))
            part = jnp.dot(
                jnp.concatenate(left, 1),
                jnp.concatenate(right, 0),
                preferred_element_type=jnp.float32,
            )
            q = plan[slots + i * CHUNKS + c]
            total[q] = total[q] + part
        return 0

    lax.fori_loop(0, plan[slots + slots // GROUP], step, 0)
    out[...] = total[...].astype(out.dtype)


def contract(plan, scale, turned, fetched, touched):
    per, side, width = fetched[0].shape
    return pl.pallas_call(
        contract_kernel,
        out_shape=jax.ShapeDtypeStruct((touched, side, width), jnp.bfloat16),
        in_specs=[SMEM, VMEM, VMEM] + [VMEM] * len(fetched),
        out_specs=VMEM,
        scratch_shapes=[
            pltpu.VMEM((len(fetched) * per, side, width), jnp.float32),
            pltpu.VMEM((touched, side, width), jnp.float32),
        ],
        compiler_params=pltpu.CompilerParams(vmem_limit_bytes=CONTRACT_MIB << 20),
        cost_estimate=pl.CostEstimate(
            flops=2 * turned.size * width, bytes_accessed=turned.size, transcendentals=0
        ),
        name="contract",
    )(plan, scale, turned, *fetched)


def merge_kernel(items_owned, per, me, heard, slot, parts, mine, *rest):
    sends, total = rest[:-1], rest[-1]
    share = mine.shape[0]
    total[...] = jnp.zeros_like(total)

    base = heard.shape[2] - per

    def add(k, _):
        for n in range(per):
            j = lax.rem(slot[heard[k, 0, base + n]], items_owned)
            total[j] = total[j] + parts[k * per + n].astype(jnp.float32)
        return 0

    lax.fori_loop(0, heard.shape[0], add, 0)
    for d in range(items_owned // share):
        first = (me[0] ^ d) * share
        for j in range(share):
            if d == 0:
                mine[j] = total[first + j]
            else:
                sends[d - 1][j] = total[first + j].astype(jnp.bfloat16)


def merge(me, heard, slot, parts, items_owned, members, per):
    side, width = parts.shape[1:]
    share = items_owned // members
    piece = lambda kind: jax.ShapeDtypeStruct((share, side, width), kind)
    return pl.pallas_call(
        functools.partial(merge_kernel, items_owned, per),
        out_shape=(piece(jnp.float32),) + (piece(jnp.bfloat16),) * (members - 1),
        in_specs=[SMEM, SMEM, SMEM, VMEM],
        out_specs=(VMEM,) * members,
        scratch_shapes=[pltpu.VMEM((items_owned, side, width), jnp.float32)],
        compiler_params=pltpu.CompilerParams(vmem_limit_bytes=12 << 20),
        name="merge",
    )(me, heard, slot, parts)


def body(
    tile_data,
    tile_user,
    tile_item,
    tile_word,
    tile_month,
    tile_live,
    user_need,
    item_need,
    user_slot,
    item_slot,
    user_factor,
    word_factor,
    month_factor,
):
    wide = lax.axis_size("wide")
    members = lax.axis_size("narrow")
    side = tile_data.shape[1]
    width = user_factor.shape[1]
    touched = item_need.shape[1]
    items_owned = item_slot.shape[0] // wide
    per_user = user_need.shape[1] // wide
    heard = lax.all_to_all(
        ask(user_need, item_need, wide), "wide", split_axis=0, concat_axis=0, tiled=True
    )
    me_wide = lax.axis_index("wide").reshape(1)
    plan = rank(me_wide, tile_live, tile_user, tile_item, touched)
    replies = answer(me_wide, heard, user_slot, user_factor.reshape(-1, side, width), per_user)
    fetched = list(replies)
    for d in reversed(range(1, wide)):
        fetched[d] = lax.ppermute(replies[d], "wide", [(k, k ^ d) for k in range(wide)])
    turned, scale = turn(
        plan,
        tile_word,
        tile_month,
        tile_data,
        word_factor,
        month_factor,
        slots_for(tile_data.shape[0], touched),
    )
    partial = contract(plan, scale, turned, fetched, touched)
    arrived = lax.all_to_all(
        partial.reshape(wide, -1, side, width), "wide", split_axis=0, concat_axis=0, tiled=True
    ).reshape(-1, side, width)
    me = lax.axis_index("narrow").reshape(1)
    pieces = merge(me, heard, item_slot, arrived, items_owned, members, touched // wide)
    rows = pieces[0]
    for d in range(1, members):
        got = lax.ppermute(pieces[d], "narrow", [(n, n ^ d) for n in range(members)])
        rows = rows + got.astype(jnp.float32)
    return rows.reshape(-1, width)


def solution(mesh):
    return jax.shard_map(
        body,
        mesh=mesh,
        in_specs=(
            P(("wide", "narrow"), None, None),
            P(("wide", "narrow")),
            P(("wide", "narrow")),
            P(("wide", "narrow")),
            P(("wide", "narrow")),
            P(("wide", "narrow")),
            P(("wide", "narrow"), None),
            P(("wide", "narrow"), None),
            P(),
            P(),
            P("wide", None),
            P(),
            P(),
        ),
        out_specs=P(("wide", "narrow"), None),
        check_vma=False,
    )
```

```python
import functools

import jax
import jax.numpy as jnp
from jax import lax
from jax.experimental import pallas as pl
from jax.experimental.pallas import tpu as pltpu
from jax.sharding import PartitionSpec as P

CONTRACT_MIB = 12
ANSWER_MIB = 12
RANK_MIB = 63
TURN_MIB = 12
TURN = 32
PADS = 8
GROUP = 4
CHUNKS = 12
SMEM = pl.BlockSpec(memory_space=pltpu.SMEM)
VMEM = pl.BlockSpec(memory_space=pltpu.VMEM)
HBM = pl.BlockSpec(memory_space=pltpu.HBM)


def rank_kernel(slots, touched, me, live, user, item, plan):
    tile_count = item.shape[0]
    dump = slots - 16
    iota = lambda shape, dim: lax.broadcasted_iota(jnp.int32, shape, dim)
    as_half = lambda mask: jnp.where(mask, 1.0, 0.0).astype(jnp.bfloat16)
    lane = iota((1, tile_count), 1)
    alive = lane < live[...].reshape(1, 1)
    one = jnp.where((iota((touched, tile_count), 0) == item[...].reshape(1, tile_count)) & alive, 1.0, 0.0)
    before = as_half(iota((tile_count, tile_count), 0) < iota((tile_count, tile_count), 1))
    earlier = jnp.dot(one.astype(jnp.bfloat16), before, preferred_element_type=jnp.float32)
    count = jnp.sum(one, axis=1, keepdims=True)
    chunks = jnp.floor((count + (GROUP - 1)) * (1.0 / GROUP))
    offset = GROUP * jnp.dot(
        as_half(iota((touched, touched), 1) < iota((touched, touched), 0)),
        jnp.broadcast_to(chunks, (touched, 128)).astype(jnp.bfloat16),
        preferred_element_type=jnp.float32,
    )[:, :1]
    here = jnp.sum(one * (earlier + offset), axis=0, keepdims=True).astype(jnp.int32)
    place = jnp.where(alive, here, dump + lax.rem(lane, 16))
    users = lax.dot_general(
        jnp.broadcast_to(user[...].reshape(1, tile_count), (8, tile_count)).astype(jnp.float32).astype(jnp.bfloat16),
        as_half(iota((slots, tile_count), 0) == place),
        (((1,), (1,)), ((), ())),
        preferred_element_type=jnp.float32,
    )
    offset, count = offset.astype(jnp.int32), count.astype(jnp.int32)
    size = GROUP * chunks.astype(jnp.int32)
    used = jnp.sum(size, axis=0, keepdims=True)
    width = plan.shape[1]
    passed = jnp.where(GROUP * iota((touched, width), 1) >= offset + size, 1, 0)
    plan[0:1, 0:slots] = users[0:1].astype(jnp.int32)
    plan[1:2, :] = jnp.minimum(jnp.sum(passed, axis=0, keepdims=True), touched - 1)
    plan[2:3, 0:tile_count] = place
    plan[3:4, :] = used + iota((1, width), 1)
    plan[4:5, :] = jnp.broadcast_to(used, (1, width))
    plan[5:6, :] = jnp.broadcast_to(me[0], (1, width))
    column = iota((touched, 128), 1)
    plan[PADS : PADS + touched, 0:128] = jnp.where(
        column < size - count, offset + count + column, dump + lax.rem(column, 16)
    )


def slots_for(tile_count, touched):
    per_step = GROUP * CHUNKS
    return -(-(tile_count + touched * (GROUP - 1)) // per_step) * per_step + per_step + 16


def rank(me, live, user, item, touched):
    slots = slots_for(user.shape[0], touched)
    return pl.pallas_call(
        functools.partial(rank_kernel, slots, touched),
        out_shape=jax.ShapeDtypeStruct((PADS + touched, -(-slots // 128) * 128), jnp.int32),
        in_specs=[SMEM, VMEM, VMEM, VMEM],
        out_specs=VMEM,
        compiler_params=pltpu.CompilerParams(vmem_limit_bytes=RANK_MIB << 20),
        cost_estimate=pl.CostEstimate(flops=1 << 33, bytes_accessed=1 << 25, transcendentals=0),
        name="rank",
    )(me, live, user, item)


def turn_kernel(plan, word, month, tiles, words, months, turned, scale, word_rows, month_rows):
    tile_count = tiles.shape[0]
    word_rows[...] = words[...].astype(jnp.float32)
    month_rows[...] = months[...].astype(jnp.float32)
    nothing = jnp.zeros(turned.shape[1:], turned.dtype)
    no_scale = jnp.zeros((1, scale.shape[1]), scale.dtype)

    def clear(p):
        turned[p] = nothing
        scale[pl.ds(p, 1), :] = no_scale

    def clear_item(q, _):
        for j in range(GROUP - 1):
            clear(plan[PADS + q, j])
        return 0

    lax.fori_loop(0, plan.shape[0] - PADS, clear_item, 0)

    def clear_rest(n, _):
        clear(plan[3, n])
        return 0

    lax.fori_loop(0, GROUP * (CHUNKS - 1), clear_rest, 0, unroll=4)

    def put(c, _):
        for n in range(TURN):
            t = c * TURN + n
            p = plan[2, t]
            turned[p] = tiles[t].T
            scale[pl.ds(p, 1), :] = (
                word_rows[pl.ds(word[t], 1), :] * month_rows[pl.ds(month[t], 1), :]
            )
        return 0

    lax.fori_loop(0, tile_count // TURN, put, 0)


def turn(plan, word, month, tiles, words, months, slots):
    side = tiles.shape[1]
    width = words.shape[1]
    return pl.pallas_call(
        turn_kernel,
        out_shape=(
            jax.ShapeDtypeStruct((slots, side, side), tiles.dtype),
            jax.ShapeDtypeStruct((slots, width), jnp.float32),
        ),
        in_specs=[SMEM, SMEM, SMEM, VMEM, VMEM, VMEM],
        out_specs=(VMEM, VMEM),
        scratch_shapes=[
            pltpu.VMEM(words.shape, jnp.float32),
            pltpu.VMEM(months.shape, jnp.float32),
        ],
        compiler_params=pltpu.CompilerParams(vmem_limit_bytes=TURN_MIB << 20),
        cost_estimate=pl.CostEstimate(
            flops=1 << 30, bytes_accessed=4 * tiles.size, transcendentals=0
        ),
        name="turn",
    )(plan, word, month, tiles, words, months)


def answer_kernel(owned, per, me, heard, slot, blocks, *outs):
    for d, out in enumerate(outs):
        k = me[0] ^ d
        for j in range(per):
            out[j] = blocks[lax.rem(slot[heard[k, 0, me[0] * per + j]], owned)]


def answer(me, heard, slot, blocks, per):
    owned, side, width = blocks.shape
    wide = heard.shape[0]
    return pl.pallas_call(
        functools.partial(answer_kernel, owned, per),
        out_shape=(jax.ShapeDtypeStruct((per, side, width), blocks.dtype),) * wide,
        in_specs=[SMEM, SMEM, SMEM, VMEM],
        out_specs=(VMEM,) * wide,
        compiler_params=pltpu.CompilerParams(vmem_limit_bytes=ANSWER_MIB << 20),
        cost_estimate=pl.CostEstimate(flops=1 << 33, bytes_accessed=1 << 25, transcendentals=0),
        name="answer",
    )(me, heard, slot, blocks)


def contract_kernel(plan, scale, turned, *refs):
    fetched, (out, wide_blocks, total) = refs[:-3], refs[-3:]
    per = fetched[0].shape[0]
    per_step = GROUP * CHUNKS
    me = plan[5, 0]
    for d, blocks in enumerate(fetched):
        for j in range(per):
            wide_blocks[(me ^ d) * per + j] = blocks[j].astype(jnp.float32)
    total[...] = jnp.zeros_like(total)

    def step(i, _):
        first = i * per_step
        for c in range(CHUNKS):
            left, right = [], []
            for g in range(GROUP):
                p = first + c * GROUP + g
                left.append(turned[p])
                right.append((wide_blocks[plan[0, p]] * scale[pl.ds(p, 1), :]).astype(jnp.bfloat16))
            part = jnp.dot(
                jnp.concatenate(left, 1),
                jnp.concatenate(right, 0),
                preferred_element_type=jnp.float32,
            )
            q = plan[1, i * CHUNKS + c]
            total[q] = total[q] + part
        return 0

    steps = (plan[4, 0] + per_step - 1) // per_step
    lax.fori_loop(0, steps, step, 0)
    out[...] = total[...].astype(out.dtype)


def contract(plan, scale, turned, fetched, touched):
    per, side, width = fetched[0].shape
    return pl.pallas_call(
        contract_kernel,
        out_shape=jax.ShapeDtypeStruct((touched, side, width), jnp.bfloat16),
        in_specs=[SMEM, VMEM, VMEM] + [VMEM] * len(fetched),
        out_specs=VMEM,
        scratch_shapes=[
            pltpu.VMEM((len(fetched) * per, side, width), jnp.float32),
            pltpu.VMEM((touched, side, width), jnp.float32),
        ],
        compiler_params=pltpu.CompilerParams(vmem_limit_bytes=CONTRACT_MIB << 20),
        cost_estimate=pl.CostEstimate(
            flops=2 * turned.size * width, bytes_accessed=turned.size, transcendentals=0
        ),
        name="contract",
    )(plan, scale, turned, *fetched)


def merge_kernel(items_owned, per, owner, me, heard, slot, parts, mine, *rest):
    sends, total = rest[:-1], rest[-1]
    share = mine.shape[0]
    total[...] = jnp.zeros_like(total)

    base = heard.shape[2] - per * heard.shape[0] + per * owner[0]

    def add(k, _):
        for n in range(per):
            j = lax.rem(slot[heard[k, 0, base + n]], items_owned)
            total[j] = total[j] + parts[k * per + n].astype(jnp.float32)
        return 0

    lax.fori_loop(0, heard.shape[0], add, 0)
    for d in range(items_owned // share):
        first = (me[0] ^ d) * share
        for j in range(share):
            if d == 0:
                mine[j] = total[first + j]
            else:
                sends[d - 1][j] = total[first + j].astype(jnp.bfloat16)


def merge(owner, me, heard, slot, parts, items_owned, members, per):
    side, width = parts.shape[1:]
    share = items_owned // members
    piece = lambda kind: jax.ShapeDtypeStruct((share, side, width), kind)
    return pl.pallas_call(
        functools.partial(merge_kernel, items_owned, per),
        out_shape=(piece(jnp.float32),) + (piece(jnp.bfloat16),) * (members - 1),
        in_specs=[SMEM, SMEM, SMEM, SMEM, VMEM],
        out_specs=(VMEM,) * members,
        scratch_shapes=[pltpu.VMEM((items_owned, side, width), jnp.float32)],
        compiler_params=pltpu.CompilerParams(vmem_limit_bytes=12 << 20),
        name="merge",
    )(owner, me, heard, slot, parts)


def body(
    tile_data,
    tile_user,
    tile_item,
    tile_word,
    tile_month,
    tile_live,
    user_need,
    item_need,
    user_slot,
    item_slot,
    user_factor,
    word_factor,
    month_factor,
):
    wide = lax.axis_size("wide")
    members = lax.axis_size("narrow")
    side = tile_data.shape[1]
    width = user_factor.shape[1]
    touched = item_need.shape[1]
    items_owned = item_slot.shape[0] // wide
    per_user = user_need.shape[1] // wide
    to_all = lambda row: jnp.broadcast_to(row[None], (wide, 1, row.shape[1]))
    need = jnp.concatenate([to_all(user_need), to_all(item_need)], axis=2)
    heard = lax.all_to_all(need, "wide", split_axis=0, concat_axis=0, tiled=True)
    me_wide = lax.axis_index("wide").reshape(1)
    plan = rank(me_wide, tile_live, tile_user, tile_item, touched)
    replies = answer(me_wide, heard, user_slot, user_factor.reshape(-1, side, width), per_user)
    fetched = list(replies)
    for d in reversed(range(1, wide)):
        fetched[d] = lax.ppermute(replies[d], "wide", [(k, k ^ d) for k in range(wide)])
    turned, scale = turn(
        plan,
        tile_word,
        tile_month,
        tile_data,
        word_factor,
        month_factor,
        slots_for(tile_data.shape[0], touched),
    )
    partial = contract(plan, scale, turned, fetched, touched)
    arrived = lax.all_to_all(
        partial.reshape(wide, -1, side, width), "wide", split_axis=0, concat_axis=0, tiled=True
    ).reshape(-1, side, width)
    me = lax.axis_index("narrow").reshape(1)
    pieces = merge(me_wide, me, heard, item_slot, arrived, items_owned, members, touched // wide)
    rows = pieces[0]
    for d in range(1, members):
        got = lax.ppermute(pieces[d], "narrow", [(n, n ^ d) for n in range(members)])
        rows = rows + got.astype(jnp.float32)
    return rows.reshape(-1, width)


def solution(mesh):
    return jax.shard_map(
        body,
        mesh=mesh,
        in_specs=(
            P(("wide", "narrow"), None, None),
            P(("wide", "narrow")),
            P(("wide", "narrow")),
            P(("wide", "narrow")),
            P(("wide", "narrow")),
            P(("wide", "narrow")),
            P(("wide", "narrow"), None),
            P(("wide", "narrow"), None),
            P(),
            P(),
            P("wide", None),
            P(),
            P(),
        ),
        out_specs=P(("wide", "narrow"), None),
        check_vma=False,
    )
```

```python
import functools

import jax
import jax.numpy as jnp
from jax import lax
from jax.experimental import pallas as pl
from jax.experimental.pallas import tpu as pltpu
from jax.sharding import PartitionSpec as P

CONTRACT_MIB = 12
ANSWER_MIB = 12
RANK_MIB = 63
TURN_MIB = 12
TURN = 32
GROUP = 4
CHUNKS = 12
SMEM = pl.BlockSpec(memory_space=pltpu.SMEM)
VMEM = pl.BlockSpec(memory_space=pltpu.VMEM)
HBM = pl.BlockSpec(memory_space=pltpu.HBM)


def lanes(n):
    return -(-n // 128) * 128


def rank_kernel(slots, touched, me, live, user, item, lay, work):
    tile_count = item.shape[0]
    dump = slots - 16
    iota = lambda shape, dim: lax.broadcasted_iota(jnp.int32, shape, dim)
    as_half = lambda mask: jnp.where(mask, 1.0, 0.0).astype(jnp.bfloat16)
    chunks_of = lambda n: jnp.floor((n + (GROUP - 1)) * (1.0 / GROUP))
    across = (((1,), (1,)), ((), ()))
    lane = iota((1, tile_count), 1)
    alive = lane < live[...].reshape(1, 1)
    one = jnp.where((iota((touched, tile_count), 0) == item[...].reshape(1, tile_count)) & alive, 1.0, 0.0)
    half = one.astype(jnp.bfloat16)
    before = as_half(iota((tile_count, tile_count), 0) < iota((tile_count, tile_count), 1))
    earlier = jnp.dot(half, before, preferred_element_type=jnp.float32)
    chunks = chunks_of(jnp.sum(one, axis=1, keepdims=True))
    small = (touched, touched)
    offset = GROUP * jnp.dot(
        as_half(iota(small, 1) < iota(small, 0)),
        jnp.broadcast_to(chunks, (touched, 128)).astype(jnp.bfloat16),
        preferred_element_type=jnp.float32,
    )[:, :1]
    here = jnp.sum(one * (earlier + offset), axis=0, keepdims=True).astype(jnp.int32)
    place = jnp.where(alive, here, dump + lax.rem(lane, 16))
    count_row = lax.dot_general(
        jnp.ones((8, tile_count), jnp.bfloat16), half, across, preferred_element_type=jnp.float32
    )
    offset_row = GROUP * jnp.dot(
        chunks_of(count_row).astype(jnp.bfloat16),
        as_half(iota(small, 0) < iota(small, 1)),
        preferred_element_type=jnp.float32,
    )
    at = lanes(tile_count)
    lay[:, 0:tile_count] = place
    lay[:, at : at + touched] = count_row[0:1].astype(jnp.int32)
    at += lanes(touched)
    lay[:, at : at + touched] = offset_row[0:1].astype(jnp.int32)
    user_row = jnp.broadcast_to(user[...].reshape(1, tile_count), (8, tile_count))
    users = lax.dot_general(
        user_row.astype(jnp.float32).astype(jnp.bfloat16),
        as_half(iota((slots, tile_count), 0) == place),
        across,
        preferred_element_type=jnp.float32,
    )
    end = (offset + GROUP * chunks).astype(jnp.int32)
    used = jnp.sum(GROUP * chunks, axis=0, keepdims=True).astype(jnp.int32)
    width = lanes(slots // GROUP)
    passed = jnp.where(GROUP * iota((touched, width), 1) >= end, 1, 0)
    work[:, 0:slots] = users[0:1].astype(jnp.int32)
    at = lanes(slots)
    work[:, at : at + width] = jnp.minimum(jnp.sum(passed, axis=0, keepdims=True), touched - 1)
    at += width
    work[:, at : at + 128] = jnp.broadcast_to(used, (1, 128))
    work[:, at + 128 : at + 256] = jnp.broadcast_to(me[0], (1, 128))


def slots_for(tile_count, touched):
    per_step = GROUP * CHUNKS
    return -(-(tile_count + touched * (GROUP - 1)) // per_step) * per_step + per_step + 16


def rank(me, live, user, item, touched):
    tile_count = user.shape[0]
    slots = slots_for(tile_count, touched)
    row = lambda n: jax.ShapeDtypeStruct((1, n), jnp.int32)
    return pl.pallas_call(
        functools.partial(rank_kernel, slots, touched),
        out_shape=(
            row(lanes(tile_count) + 2 * lanes(touched)),
            row(lanes(slots) + lanes(slots // GROUP) + 256),
        ),
        in_specs=[SMEM, VMEM, VMEM, VMEM],
        out_specs=(VMEM, VMEM),
        compiler_params=pltpu.CompilerParams(vmem_limit_bytes=RANK_MIB << 20),
        cost_estimate=pl.CostEstimate(flops=1 << 33, bytes_accessed=1 << 25, transcendentals=0),
        name="rank",
    )(me, live, user, item)


def turn_kernel(touched, lay, word, month, tiles, words, months, turned, scale, word_rows, month_rows):
    tile_count = tiles.shape[0]
    dump = turned.shape[0] - 16
    counts = lanes(tile_count)
    offsets = counts + lanes(touched)
    word_rows[...] = words[...].astype(jnp.float32)
    month_rows[...] = months[...].astype(jnp.float32)
    nothing = jnp.zeros(turned.shape[1:], turned.dtype)
    no_scale = jnp.zeros((1, scale.shape[1]), scale.dtype)

    def clear(p):
        turned[p] = nothing
        scale[pl.ds(p, 1), :] = no_scale

    def clear_item(q, _):
        end = lay[0, offsets + q] + lay[0, counts + q]
        for j in range(GROUP - 1):
            clear(jnp.where(lax.rem(end + j, GROUP) > lax.rem(end + GROUP - 1, GROUP), end + j, dump + j))
        return lax.div(end + GROUP - 1, GROUP) * GROUP

    used = lax.fori_loop(0, touched, clear_item, 0)

    def clear_rest(n, _):
        clear(used + n)
        return 0

    lax.fori_loop(0, GROUP * (CHUNKS - 1), clear_rest, 0, unroll=4)

    def put(c, _):
        for n in range(TURN):
            t = c * TURN + n
            p = lay[0, t]
            turned[p] = tiles[t].T
            scale[pl.ds(p, 1), :] = (
                word_rows[pl.ds(word[t], 1), :] * month_rows[pl.ds(month[t], 1), :]
            )
        return 0

    lax.fori_loop(0, tile_count // TURN, put, 0)


def turn(lay, word, month, tiles, words, months, slots, touched):
    side = tiles.shape[1]
    width = words.shape[1]
    return pl.pallas_call(
        functools.partial(turn_kernel, touched),
        out_shape=(
            jax.ShapeDtypeStruct((slots, side, side), tiles.dtype),
            jax.ShapeDtypeStruct((slots, width), jnp.float32),
        ),
        in_specs=[SMEM, SMEM, SMEM, VMEM, VMEM, VMEM],
        out_specs=(VMEM, VMEM),
        scratch_shapes=[
            pltpu.VMEM(words.shape, jnp.float32),
            pltpu.VMEM(months.shape, jnp.float32),
        ],
        compiler_params=pltpu.CompilerParams(vmem_limit_bytes=TURN_MIB << 20),
        cost_estimate=pl.CostEstimate(
            flops=1 << 30, bytes_accessed=4 * tiles.size, transcendentals=0
        ),
        name="turn",
    )(lay, word, month, tiles, words, months)


def ask_kernel(user_need, item_need, need):
    wide, _, both = need.shape
    users = user_need.shape[1]
    need[:, :, 0:users] = jnp.broadcast_to(user_need[...][None], (wide, 1, users))
    need[:, :, users:both] = jnp.broadcast_to(item_need[...][None], (wide, 1, both - users))


def ask(user_need, item_need, wide):
    both = user_need.shape[1] + item_need.shape[1]
    return pl.pallas_call(
        ask_kernel,
        out_shape=jax.ShapeDtypeStruct((wide, 1, both), jnp.int32),
        in_specs=[VMEM, VMEM],
        out_specs=VMEM,
        compiler_params=pltpu.CompilerParams(vmem_limit_bytes=63 << 20),
        name="ask",
    )(user_need, item_need)


def answer_kernel(owned, per, me, heard, slot, blocks, *outs):
    for d, out in enumerate(outs):
        k = me[0] ^ d
        for j in range(per):
            out[j] = blocks[lax.rem(slot[heard[k, 0, me[0] * per + j]], owned)]


def answer(me, heard, slot, blocks, per):
    owned, side, width = blocks.shape
    wide = heard.shape[0]
    return pl.pallas_call(
        functools.partial(answer_kernel, owned, per),
        out_shape=(jax.ShapeDtypeStruct((per, side, width), blocks.dtype),) * wide,
        in_specs=[SMEM, SMEM, SMEM, VMEM],
        out_specs=(VMEM,) * wide,
        compiler_params=pltpu.CompilerParams(vmem_limit_bytes=ANSWER_MIB << 20),
        cost_estimate=pl.CostEstimate(flops=1 << 33, bytes_accessed=1 << 25, transcendentals=0),
        name="answer",
    )(me, heard, slot, blocks)


def contract_kernel(work, scale, turned, *refs):
    fetched, (out, wide_blocks, total) = refs[:-3], refs[-3:]
    per = fetched[0].shape[0]
    per_step = GROUP * CHUNKS
    items = lanes(scale.shape[0])
    used = items + lanes(scale.shape[0] // GROUP)
    me = work[0, used + 128]
    for d, blocks in enumerate(fetched):
        for j in range(per):
            wide_blocks[(me ^ d) * per + j] = blocks[j].astype(jnp.float32)
    total[...] = jnp.zeros_like(total)

    def step(i, _):
        first = i * per_step
        for c in range(CHUNKS):
            left, right = [], []
            for g in range(GROUP):
                p = first + c * GROUP + g
                left.append(turned[p])
                right.append((wide_blocks[work[0, p]] * scale[pl.ds(p, 1), :]).astype(jnp.bfloat16))
            part = jnp.dot(
                jnp.concatenate(left, 1),
                jnp.concatenate(right, 0),
                preferred_element_type=jnp.float32,
            )
            q = work[0, items + i * CHUNKS + c]
            total[q] = total[q] + part
        return 0

    steps = (work[0, used] + per_step - 1) // per_step
    lax.fori_loop(0, steps, step, 0)
    out[...] = total[...].astype(out.dtype)


def contract(work, scale, turned, fetched, touched):
    per, side, width = fetched[0].shape
    return pl.pallas_call(
        contract_kernel,
        out_shape=jax.ShapeDtypeStruct((touched, side, width), jnp.bfloat16),
        in_specs=[SMEM, VMEM, VMEM] + [VMEM] * len(fetched),
        out_specs=VMEM,
        scratch_shapes=[
            pltpu.VMEM((len(fetched) * per, side, width), jnp.float32),
            pltpu.VMEM((touched, side, width), jnp.float32),
        ],
        compiler_params=pltpu.CompilerParams(vmem_limit_bytes=CONTRACT_MIB << 20),
        cost_estimate=pl.CostEstimate(
            flops=2 * turned.size * width, bytes_accessed=turned.size, transcendentals=0
        ),
        name="contract",
    )(work, scale, turned, *fetched)


def merge_kernel(items_owned, per, owner, me, heard, slot, parts, mine, *rest):
    sends, total = rest[:-1], rest[-1]
    share = mine.shape[0]
    total[...] = jnp.zeros_like(total)

    base = heard.shape[2] - per * heard.shape[0] + per * owner[0]

    def add(k, _):
        for n in range(per):
            j = lax.rem(slot[heard[k, 0, base + n]], items_owned)
            total[j] = total[j] + parts[k * per + n].astype(jnp.float32)
        return 0

    lax.fori_loop(0, heard.shape[0], add, 0)
    for d in range(items_owned // share):
        first = (me[0] ^ d) * share
        for j in range(share):
            if d == 0:
                mine[j] = total[first + j]
            else:
                sends[d - 1][j] = total[first + j].astype(jnp.bfloat16)


def merge(owner, me, heard, slot, parts, items_owned, members, per):
    side, width = parts.shape[1:]
    share = items_owned // members
    piece = lambda kind: jax.ShapeDtypeStruct((share, side, width), kind)
    return pl.pallas_call(
        functools.partial(merge_kernel, items_owned, per),
        out_shape=(piece(jnp.float32),) + (piece(jnp.bfloat16),) * (members - 1),
        in_specs=[SMEM, SMEM, SMEM, SMEM, VMEM],
        out_specs=(VMEM,) * members,
        scratch_shapes=[pltpu.VMEM((items_owned, side, width), jnp.float32)],
        compiler_params=pltpu.CompilerParams(vmem_limit_bytes=12 << 20),
        name="merge",
    )(owner, me, heard, slot, parts)


def body(
    tile_data,
    tile_user,
    tile_item,
    tile_word,
    tile_month,
    tile_live,
    user_need,
    item_need,
    user_slot,
    item_slot,
    user_factor,
    word_factor,
    month_factor,
):
    wide = lax.axis_size("wide")
    members = lax.axis_size("narrow")
    side = tile_data.shape[1]
    width = user_factor.shape[1]
    touched = item_need.shape[1]
    items_owned = item_slot.shape[0] // wide
    per_user = user_need.shape[1] // wide
    need = ask(user_need, item_need, wide)
    heard = lax.all_to_all(need, "wide", split_axis=0, concat_axis=0, tiled=True)
    me_wide = lax.axis_index("wide").reshape(1)
    lay, work = rank(me_wide, tile_live, tile_user, tile_item, touched)
    replies = answer(me_wide, heard, user_slot, user_factor.reshape(-1, side, width), per_user)
    fetched = list(replies)
    for d in reversed(range(1, wide)):
        fetched[d] = lax.ppermute(replies[d], "wide", [(k, k ^ d) for k in range(wide)])
    turned, scale = turn(
        lay,
        tile_word,
        tile_month,
        tile_data,
        word_factor,
        month_factor,
        slots_for(tile_data.shape[0], touched),
        touched,
    )
    partial = contract(work, scale, turned, fetched, touched)
    arrived = lax.all_to_all(
        partial.reshape(wide, -1, side, width), "wide", split_axis=0, concat_axis=0, tiled=True
    ).reshape(-1, side, width)
    me = lax.axis_index("narrow").reshape(1)
    pieces = merge(me_wide, me, heard, item_slot, arrived, items_owned, members, touched // wide)
    rows = pieces[0]
    for d in range(1, members):
        got = lax.ppermute(pieces[d], "narrow", [(n, n ^ d) for n in range(members)])
        rows = rows + got.astype(jnp.float32)
    return rows.reshape(-1, width)


def solution(mesh):
    return jax.shard_map(
        body,
        mesh=mesh,
        in_specs=(
            P(("wide", "narrow"), None, None),
            P(("wide", "narrow")),
            P(("wide", "narrow")),
            P(("wide", "narrow")),
            P(("wide", "narrow")),
            P(("wide", "narrow")),
            P(("wide", "narrow"), None),
            P(("wide", "narrow"), None),
            P(),
            P(),
            P("wide", None),
            P(),
            P(),
        ),
        out_specs=P(("wide", "narrow"), None),
        check_vma=False,
    )
```

```python
import functools

import jax
import jax.numpy as jnp
from jax import lax
from jax.experimental import pallas as pl
from jax.experimental.pallas import tpu as pltpu
from jax.sharding import PartitionSpec as P

CONTRACT_MIB = 12
ANSWER_MIB = 12
RANK_MIB = 63
TURN_MIB = 12
TURN = 64
GROUP = 2
CHUNKS = 28
SMEM = pl.BlockSpec(memory_space=pltpu.SMEM)
VMEM = pl.BlockSpec(memory_space=pltpu.VMEM)
HBM = pl.BlockSpec(memory_space=pltpu.HBM)


def lanes(n):
    return -(-n // 128) * 128


def rank_kernel(slots, touched, me, live, user, item, lay, work):
    tile_count = item.shape[0]
    dump = slots - 16
    iota = lambda shape, dim: lax.broadcasted_iota(jnp.int32, shape, dim)
    as_half = lambda mask: jnp.where(mask, 1.0, 0.0).astype(jnp.bfloat16)
    chunks_of = lambda n: jnp.floor((n + (GROUP - 1)) * (1.0 / GROUP))
    across = (((1,), (1,)), ((), ()))
    lane = iota((1, tile_count), 1)
    alive = lane < live[...].reshape(1, 1)
    one = jnp.where((iota((touched, tile_count), 0) == item[...].reshape(1, tile_count)) & alive, 1.0, 0.0)
    half = one.astype(jnp.bfloat16)
    before = as_half(iota((tile_count, tile_count), 0) < iota((tile_count, tile_count), 1))
    earlier = jnp.dot(half, before, preferred_element_type=jnp.float32)
    chunks = chunks_of(jnp.sum(one, axis=1, keepdims=True))
    small = (touched, touched)
    offset = GROUP * jnp.dot(
        as_half(iota(small, 1) < iota(small, 0)),
        jnp.broadcast_to(chunks, (touched, 128)).astype(jnp.bfloat16),
        preferred_element_type=jnp.float32,
    )[:, :1]
    here = jnp.sum(one * (earlier + offset), axis=0, keepdims=True).astype(jnp.int32)
    place = jnp.where(alive, here, dump + lax.rem(lane, 16))
    count_row = lax.dot_general(
        jnp.ones((8, tile_count), jnp.bfloat16), half, across, preferred_element_type=jnp.float32
    )
    offset_row = GROUP * jnp.dot(
        chunks_of(count_row).astype(jnp.bfloat16),
        as_half(iota(small, 0) < iota(small, 1)),
        preferred_element_type=jnp.float32,
    )
    at = lanes(tile_count)
    lay[:, 0:tile_count] = place
    lay[:, at : at + touched] = count_row[0:1].astype(jnp.int32)
    at += lanes(touched)
    lay[:, at : at + touched] = offset_row[0:1].astype(jnp.int32)
    user_row = jnp.broadcast_to(user[...].reshape(1, tile_count), (8, tile_count))
    users = lax.dot_general(
        user_row.astype(jnp.float32).astype(jnp.bfloat16),
        as_half(iota((slots, tile_count), 0) == place),
        across,
        preferred_element_type=jnp.float32,
    )
    end = (offset + GROUP * chunks).astype(jnp.int32)
    used = jnp.sum(GROUP * chunks, axis=0, keepdims=True).astype(jnp.int32)
    width = lanes(slots // GROUP)
    passed = jnp.where(GROUP * iota((touched, width), 1) >= end, 1, 0)
    work[:, 0:slots] = users[0:1].astype(jnp.int32)
    at = lanes(slots)
    work[:, at : at + width] = jnp.minimum(jnp.sum(passed, axis=0, keepdims=True), touched - 1)
    at += width
    work[:, at : at + 128] = jnp.broadcast_to(used, (1, 128))
    work[:, at + 128 : at + 256] = jnp.broadcast_to(me[0], (1, 128))


def slots_for(tile_count, touched):
    per_step = GROUP * CHUNKS
    return -(-(tile_count + touched * (GROUP - 1)) // per_step) * per_step + per_step + 16


def rank(me, live, user, item, touched):
    tile_count = user.shape[0]
    slots = slots_for(tile_count, touched)
    row = lambda n: jax.ShapeDtypeStruct((1, n), jnp.int32)
    return pl.pallas_call(
        functools.partial(rank_kernel, slots, touched),
        out_shape=(
            row(lanes(tile_count) + 2 * lanes(touched)),
            row(lanes(slots) + lanes(slots // GROUP) + 256),
        ),
        in_specs=[SMEM, VMEM, VMEM, VMEM],
        out_specs=(VMEM, VMEM),
        compiler_params=pltpu.CompilerParams(vmem_limit_bytes=RANK_MIB << 20),
        cost_estimate=pl.CostEstimate(flops=1 << 33, bytes_accessed=1 << 25, transcendentals=0),
        name="rank",
    )(me, live, user, item)


def turn_kernel(touched, lay, word, month, tiles, words, months, turned, scale, word_rows, month_rows):
    tile_count = tiles.shape[0]
    dump = turned.shape[0] - 16
    counts = lanes(tile_count)
    offsets = counts + lanes(touched)
    word_rows[...] = words[...].astype(jnp.float32)
    month_rows[...] = months[...].astype(jnp.float32)
    nothing = jnp.zeros(turned.shape[1:], turned.dtype)
    no_scale = jnp.zeros((1, scale.shape[1]), scale.dtype)

    def clear(p):
        turned[p] = nothing
        scale[pl.ds(p, 1), :] = no_scale

    def clear_item(q, _):
        end = lay[0, offsets + q] + lay[0, counts + q]
        for j in range(GROUP - 1):
            clear(jnp.where(lax.rem(end + j, GROUP) > lax.rem(end + GROUP - 1, GROUP), end + j, dump + j))
        return lax.div(end + GROUP - 1, GROUP) * GROUP

    used = lax.fori_loop(0, touched, clear_item, 0)

    def clear_rest(n, _):
        clear(used + n)
        return 0

    lax.fori_loop(0, GROUP * (CHUNKS - 1), clear_rest, 0, unroll=4)

    def put(c, _):
        for n in range(TURN):
            t = c * TURN + n
            p = lay[0, t]
            turned[p] = tiles[t].T
            scale[pl.ds(p, 1), :] = (
                word_rows[pl.ds(word[t], 1), :] * month_rows[pl.ds(month[t], 1), :]
            )
        return 0

    lax.fori_loop(0, tile_count // TURN, put, 0)


def turn(lay, word, month, tiles, words, months, slots, touched):
    side = tiles.shape[1]
    width = words.shape[1]
    return pl.pallas_call(
        functools.partial(turn_kernel, touched),
        out_shape=(
            jax.ShapeDtypeStruct((slots, side, side), tiles.dtype),
            jax.ShapeDtypeStruct((slots, width), jnp.float32),
        ),
        in_specs=[SMEM, SMEM, SMEM, VMEM, VMEM, VMEM],
        out_specs=(VMEM, VMEM),
        scratch_shapes=[
            pltpu.VMEM(words.shape, jnp.float32),
            pltpu.VMEM(months.shape, jnp.float32),
        ],
        compiler_params=pltpu.CompilerParams(vmem_limit_bytes=TURN_MIB << 20),
        cost_estimate=pl.CostEstimate(
            flops=1 << 30, bytes_accessed=4 * tiles.size, transcendentals=0
        ),
        name="turn",
    )(lay, word, month, tiles, words, months)


def ask_kernel(user_need, item_need, need):
    wide, _, both = need.shape
    users = user_need.shape[1]
    need[:, :, 0:users] = jnp.broadcast_to(user_need[...][None], (wide, 1, users))
    need[:, :, users:both] = jnp.broadcast_to(item_need[...][None], (wide, 1, both - users))


def ask(user_need, item_need, wide):
    both = user_need.shape[1] + item_need.shape[1]
    return pl.pallas_call(
        ask_kernel,
        out_shape=jax.ShapeDtypeStruct((wide, 1, both), jnp.int32),
        in_specs=[VMEM, VMEM],
        out_specs=VMEM,
        compiler_params=pltpu.CompilerParams(vmem_limit_bytes=63 << 20),
        name="ask",
    )(user_need, item_need)


def answer_kernel(owned, per, me, heard, slot, blocks, *outs):
    for d, out in enumerate(outs):
        k = me[0] ^ d
        for j in range(per):
            out[j] = blocks[lax.rem(slot[heard[k, 0, me[0] * per + j]], owned)]


def answer(me, heard, slot, blocks, per):
    owned, side, width = blocks.shape
    wide = heard.shape[0]
    return pl.pallas_call(
        functools.partial(answer_kernel, owned, per),
        out_shape=(jax.ShapeDtypeStruct((per, side, width), blocks.dtype),) * wide,
        in_specs=[SMEM, SMEM, SMEM, VMEM],
        out_specs=(VMEM,) * wide,
        compiler_params=pltpu.CompilerParams(vmem_limit_bytes=ANSWER_MIB << 20),
        cost_estimate=pl.CostEstimate(flops=1 << 33, bytes_accessed=1 << 25, transcendentals=0),
        name="answer",
    )(me, heard, slot, blocks)


def contract_kernel(work, scale, turned, *refs):
    fetched, (out, wide_blocks, total) = refs[:-3], refs[-3:]
    per = fetched[0].shape[0]
    per_step = GROUP * CHUNKS
    items = lanes(scale.shape[0])
    used = items + lanes(scale.shape[0] // GROUP)
    me = work[0, used + 128]
    for d, blocks in enumerate(fetched):
        for j in range(per):
            wide_blocks[(me ^ d) * per + j] = blocks[j].astype(jnp.float32)
    total[...] = jnp.zeros_like(total)

    def step(i, _):
        first = i * per_step
        for c in range(CHUNKS):
            left, right = [], []
            for g in range(GROUP):
                p = first + c * GROUP + g
                left.append(turned[p])
                right.append((wide_blocks[work[0, p]] * scale[pl.ds(p, 1), :]).astype(jnp.bfloat16))
            part = jnp.dot(
                jnp.concatenate(left, 1),
                jnp.concatenate(right, 0),
                preferred_element_type=jnp.float32,
            )
            q = work[0, items + i * CHUNKS + c]
            total[q] = total[q] + part
        return 0

    steps = (work[0, used] + per_step - 1) // per_step
    lax.fori_loop(0, steps, step, 0)
    out[...] = total[...].astype(out.dtype)


def contract(work, scale, turned, fetched, touched):
    per, side, width = fetched[0].shape
    return pl.pallas_call(
        contract_kernel,
        out_shape=jax.ShapeDtypeStruct((touched, side, width), jnp.bfloat16),
        in_specs=[SMEM, VMEM, VMEM] + [VMEM] * len(fetched),
        out_specs=VMEM,
        scratch_shapes=[
            pltpu.VMEM((len(fetched) * per, side, width), jnp.float32),
            pltpu.VMEM((touched, side, width), jnp.float32),
        ],
        compiler_params=pltpu.CompilerParams(vmem_limit_bytes=CONTRACT_MIB << 20),
        cost_estimate=pl.CostEstimate(
            flops=2 * turned.size * width, bytes_accessed=turned.size, transcendentals=0
        ),
        name="contract",
    )(work, scale, turned, *fetched)


def merge_kernel(items_owned, per, owner, me, heard, slot, parts, mine, *rest):
    sends, total = rest[:-1], rest[-1]
    share = mine.shape[0]
    total[...] = jnp.zeros_like(total)

    base = heard.shape[2] - per * heard.shape[0] + per * owner[0]

    def add(k, _):
        for n in range(per):
            j = lax.rem(slot[heard[k, 0, base + n]], items_owned)
            total[j] = total[j] + parts[k * per + n].astype(jnp.float32)
        return 0

    lax.fori_loop(0, heard.shape[0], add, 0)
    for d in range(items_owned // share):
        first = (me[0] ^ d) * share
        for j in range(share):
            if d == 0:
                mine[j] = total[first + j]
            else:
                sends[d - 1][j] = total[first + j].astype(jnp.bfloat16)


def merge(owner, me, heard, slot, parts, items_owned, members, per):
    side, width = parts.shape[1:]
    share = items_owned // members
    piece = lambda kind: jax.ShapeDtypeStruct((share, side, width), kind)
    return pl.pallas_call(
        functools.partial(merge_kernel, items_owned, per),
        out_shape=(piece(jnp.float32),) + (piece(jnp.bfloat16),) * (members - 1),
        in_specs=[SMEM, SMEM, SMEM, SMEM, VMEM],
        out_specs=(VMEM,) * members,
        scratch_shapes=[pltpu.VMEM((items_owned, side, width), jnp.float32)],
        compiler_params=pltpu.CompilerParams(vmem_limit_bytes=12 << 20),
        name="merge",
    )(owner, me, heard, slot, parts)


def body(
    tile_data,
    tile_user,
    tile_item,
    tile_word,
    tile_month,
    tile_live,
    user_need,
    item_need,
    user_slot,
    item_slot,
    user_factor,
    word_factor,
    month_factor,
):
    wide = lax.axis_size("wide")
    members = lax.axis_size("narrow")
    side = tile_data.shape[1]
    width = user_factor.shape[1]
    touched = item_need.shape[1]
    items_owned = item_slot.shape[0] // wide
    per_user = user_need.shape[1] // wide
    need = ask(user_need, item_need, wide)
    heard = lax.all_to_all(need, "wide", split_axis=0, concat_axis=0, tiled=True)
    me_wide = lax.axis_index("wide").reshape(1)
    lay, work = rank(me_wide, tile_live, tile_user, tile_item, touched)
    replies = answer(me_wide, heard, user_slot, user_factor.reshape(-1, side, width), per_user)
    fetched = list(replies)
    for d in reversed(range(1, wide)):
        fetched[d] = lax.ppermute(replies[d], "wide", [(k, k ^ d) for k in range(wide)])
    turned, scale = turn(
        lay,
        tile_word,
        tile_month,
        tile_data,
        word_factor,
        month_factor,
        slots_for(tile_data.shape[0], touched),
        touched,
    )
    partial = contract(work, scale, turned, fetched, touched)
    arrived = lax.all_to_all(
        partial.reshape(wide, -1, side, width), "wide", split_axis=0, concat_axis=0, tiled=True
    ).reshape(-1, side, width)
    me = lax.axis_index("narrow").reshape(1)
    pieces = merge(me_wide, me, heard, item_slot, arrived, items_owned, members, touched // wide)
    rows = pieces[0]
    for d in range(1, members):
        got = lax.ppermute(pieces[d], "narrow", [(n, n ^ d) for n in range(members)])
        rows = rows + got.astype(jnp.float32)
    return rows.reshape(-1, width)


def solution(mesh):
    return jax.shard_map(
        body,
        mesh=mesh,
        in_specs=(
            P(("wide", "narrow"), None, None),
            P(("wide", "narrow")),
            P(("wide", "narrow")),
            P(("wide", "narrow")),
            P(("wide", "narrow")),
            P(("wide", "narrow")),
            P(("wide", "narrow"), None),
            P(("wide", "narrow"), None),
            P(),
            P(),
            P("wide", None),
            P(),
            P(),
        ),
        out_specs=P(("wide", "narrow"), None),
        check_vma=False,
    )
```
